32 devices in a mesh: grp: 2 (over x), seq: 8 (over z, y), head: 2 (over core).
Axes of the slice: x: 2, y: 2, z: 4, core: 2. Of those that a mesh axis runs over, the one named last changes fastest.
Arguments:
- query: bfloat16 [2048, 4096], P(('grp', 'seq'), 'head'), parts along dimension 0, may hold values from -6 to 6
- keys: bfloat16 [2048, 4096], P(('grp', 'seq'), 'head'), parts along dimension 0, may hold values from -6 to 6
- values: bfloat16 [2048, 4096], P(('grp', 'seq'), 'head'), parts along dimension 0, may hold values from -6 to 6
- resid: bfloat16 [2048, 3072], P(('grp', 'seq'), 'head'), parts along dimension 0, may hold values from -6 to 6
- attn_gain: float32 [4096], P('head'), may hold values from 0.2 to 1.8
- out_weight: bfloat16 [4096, 3072], P('head', 'seq'), may hold values from -0.09375 to 0.09375
- moe_gain: float32 [3072], replicated, may hold values from 0.2 to 1.8
- routes: int32 [2048, 2], P(('grp', 'seq')), parts along dimension 0, may hold values from 0 to 7, all different within a row; in each aligned block of 128 rows (0 to 127, 128 to 255, ...) at most 36 rows name the same one
- route_weights: float32 [2048, 2], P(('grp', 'seq')), parts along dimension 0, may hold values from 0.2 to 1
- w_gate: bfloat16 [3072, 36864], P(None, ('seq', 'head')), may hold values from -0.109375 to 0.109375
- w_up: bfloat16 [3072, 36864], P(None, ('seq', 'head')), may hold values from -0.109375 to 0.109375
- w_down: bfloat16 [36864, 3072], P(('seq', 'head')), may hold values from -0.09375 to 0.09375
Outputs:
- mixed: bfloat16 [2048, 3072], P(('grp', 'seq'), 'head'), parts along dimension 0
The draws below stay inside these ranges and needn't reach their ends.
There are 2 independent parts, one for each index of `grp`. The reference program is written for one: setup_inputs(seed, part) draws one part's arguments, and reference() takes and returns one part's arrays. A program takes and returns all parts, laid end to end along the dimension named above; an argument that names none is the same for every part. Nothing has to cross between parts.
Inputs may be any that keep to these rules, and one draw needn't show every extreme that they name: A token's 2 experts differ. Within each aligned block of 128 tokens no expert is named by more than 36 routes, and in every draw some expert is named by exactly 36 routes of some block.
All inputs are finite; a program needn't handle non-finite values.
Results may differ from the reference program's by a relative error of at most 0.015.
Values may be sent and summed in bfloat16 or wider, within the bound.
A program may use at most 128 MiB of HBM per device.

```python
import math
import jax
import jax.numpy as jnp
import numpy as np
from jax import lax

D = 3072
HEADS = 32
HD = 128
EXPERTS = 8
FF = 4608
TOP = 2
TOK_DEV = 128
TOKENS = 1024
CAP = 36
SLICES = 2
FF_DEV = 2304


def steps_of(rng, shape, split, smallest, high):
    factor_of = 1.0
    for position, parts in split:
        draws = jax.random.uniform(jax.random.fold_in(jax.random.fold_in(rng, 6), position), (parts,), jnp.float32, smallest / len(split), high / len(split))
        factor_of = factor_of * jnp.repeat(jnp.exp(draws), shape[position] // parts).reshape((-1,) + (1,) * (len(shape) - 1 - position))
    return factor_of


def shared_out(key, own, number, rows, count, top, reach, skew):
    sequence = jax.random.permutation(key, count)
    crowded, ordinary = portions_of(count, rows * top, reach, skew, True), portions_of(count, rows * top, reach, skew, False)
    places = jnp.arange(count)

    def named(lengths, turn):
        used = int((lengths > 0).sum())
        fixed = max(1, used // 4)
        passed = fixed + (places - fixed + turn * (used - fixed)) % max(1, count - fixed)
        return jnp.zeros((count,), jnp.int32).at[sequence[jnp.where(places < fixed, places, passed)]].set(jnp.asarray(lengths, jnp.int32))

    lengths = jnp.where(number % 4 == 0, named(crowded, number // 4), named(ordinary, number - number // 4 - 1))
    mixed = jax.random.permutation(jax.random.fold_in(own, 3), count)
    donor, taker = mixed[0:count // 2 * 2:2], mixed[1:count // 2 * 2:2]
    slack = jnp.minimum(lengths[donor] - 1, reach - lengths[taker]) // 2
    slack = jnp.where((donor == sequence[0]) | (taker == sequence[0]) | (lengths[taker] == 0), 0, jnp.maximum(slack, 0))
    passed = jax.random.randint(jax.random.fold_in(own, 4), (count // 2,), 0, 1 << 20) % (slack + 1)
    lengths = lengths.at[donor].add(-passed).at[taker].add(passed)
    members = jnp.searchsorted(jnp.cumsum(lengths), jnp.arange(rows * top), side="right").astype(jnp.int32)
    table = members.reshape(top, rows).T
    table = table[jax.random.permutation(jax.random.fold_in(own, 1), rows)]
    turn = jax.random.randint(jax.random.fold_in(own, 2), (rows, 1), 0, top)
    return jnp.take_along_axis(table, (jnp.arange(top)[None, :] + turn) % top, axis=1)


def portions_of(amount, total, most, slope, full):
    portions = [(1 << 20) // math.isqrt(standing ** slope) + 1 for standing in range(1, amount + 1)]
    largest = most if full else min(most, max(-(-total // amount), total * portions[0] // sum(portions)))
    least = 1 if total - largest >= amount - 1 else 0
    holding, spare = [largest] + [least] * (amount - 1), total - largest - least * (amount - 1)
    while spare > 0:
        free = [i for i in range(1, amount) if holding[i] < largest] or [i for i in range(1, amount) if holding[i] < most]
        mass, left = sum([portions[i] for i in free]), spare
        for i in free:
            extra = min(most - holding[i], max(1, left * portions[i] // mass), spare)
            holding[i] = holding[i] + extra
            spare = spare - extra
    return np.array(holding)


def centred(key, extent, scale, bound, pieces=(), kind=jnp.bfloat16):
    drawn = scale * jax.random.normal(key, extent, jnp.float32)
    if pieces:
        drawn = drawn * steps_of(key, extent, pieces, -0.22, 0.18)
    return jnp.clip(drawn, -bound, bound).astype(kind)


def setup_inputs(seed: int = 0, part: int = 0) -> dict:
    streams_of = jax.random.split(jax.random.key(seed), 13)
    own_keys = jax.random.split(jax.random.fold_in(streams_of[12], part), 13)
    query = centred(own_keys[0], (TOKENS, HEADS * HD), 1.0, 6.0, ((0, 8), (1, 2)))
    keys = centred(own_keys[1], (TOKENS, HEADS * HD), 1.0, 6.0, ((0, 8), (1, 2)))
    values = centred(own_keys[2], (TOKENS, HEADS * HD), 1.0, 6.0, ((0, 8), (1, 2)))
    resid = centred(own_keys[3], (TOKENS, D), 1.0, 6.0, ((0, 8), (1, 2)))
    attn_gain = jnp.clip(1.0 + 0.16 * jax.random.normal(streams_of[4], (HEADS * HD,), jnp.float32), 0.2, 1.8)
    out_weight = centred(streams_of[5], (HEADS * HD, D), (HEADS * HD) ** -0.5, 0.09375, ((0, 2), (1, 8)))
    moe_gain = jnp.clip(1.0 + 0.16 * jax.random.normal(streams_of[6], (D,), jnp.float32), 0.2, 1.8)
    routes_keys = jax.random.split(jax.random.fold_in(own_keys[7], 1), TOKENS // TOK_DEV)
    routes_turns = jax.random.permutation(jax.random.fold_in(own_keys[7], 3), TOKENS // TOK_DEV)
    routes = jax.vmap(lambda own, number: shared_out(jax.random.fold_in(own_keys[7], 2), own, number, TOK_DEV, EXPERTS, TOP, CAP, 2))(routes_keys, routes_turns).reshape((TOKENS, TOP))
    route_weights = jnp.clip(0.2 + 0.8 * jax.random.uniform(own_keys[8], (TOKENS, TOP), jnp.float32) ** steps_of(own_keys[8], (TOKENS, TOP), ((0, 8),), -0.2, 0.2), 0.2, 1.0)
    w_gate = centred(streams_of[9], (D, EXPERTS * FF), D ** -0.5, 0.109375, ((1, 16),))
    w_up = centred(streams_of[10], (D, EXPERTS * FF), D ** -0.5, 0.109375, ((1, 16),))
    w_down = centred(streams_of[11], (EXPERTS * FF, D), FF ** -0.5, 0.09375, ((0, 16),))
    return dict(query=query, keys=keys, values=values, resid=resid, attn_gain=attn_gain, out_weight=out_weight, moe_gain=moe_gain, routes=routes, route_weights=route_weights, w_gate=w_gate, w_up=w_up, w_down=w_down)


EPS = 1e-06

def reference(query, keys, values, resid, attn_gain, out_weight, moe_gain, routes, route_weights, w_gate, w_up, w_down):
    blocks = TOKENS // TOK_DEV
    query_four_dims = query.astype(jnp.float32).reshape(blocks, TOK_DEV, HEADS, HD)
    k_four = keys.astype(jnp.float32).reshape(blocks, TOK_DEV, HEADS, HD)
    v_four = values.astype(jnp.float32).reshape(blocks, TOK_DEV, HEADS, HD)
    states = jnp.einsum('btnd,btne->bnde', k_four, v_four)
    running = jnp.cumsum(states, axis=0)
    earlier = jnp.concatenate([jnp.zeros_like(states[:1]), running[:-1]], axis=0)
    rounded_values = lax.optimization_barrier(earlier.astype(jnp.bfloat16)).astype(jnp.float32)
    inter = jnp.einsum('btnd,bnde->btne', query_four_dims, rounded_values)
    scores = jnp.einsum('btnd,bsnd->bnts', query_four_dims, k_four)
    causal = jnp.arange(TOK_DEV)[:, None] >= jnp.arange(TOK_DEV)[None, :]
    masked = lax.optimization_barrier(jnp.where(causal, scores, 0.0).astype(jnp.bfloat16)).astype(jnp.float32)
    inside_block_scores = jnp.einsum('bnts,bsne->btne', masked, v_four)
    attention = inter + inside_block_scores
    scale = lax.rsqrt(lax.optimization_barrier(jnp.mean(attention * attention, axis=-1, keepdims=True)) + EPS)
    normed = (attention * scale * attn_gain.reshape(HEADS, HD)).astype(jnp.bfloat16).reshape(TOKENS, HEADS * HD)
    projected = jnp.dot(normed, out_weight, preferred_element_type=jnp.float32)
    hidden = (resid.astype(jnp.float32) + projected).astype(jnp.bfloat16)
    wide = hidden.astype(jnp.float32)
    moe_in = (wide * lax.rsqrt(lax.optimization_barrier(jnp.mean(wide * wide, axis=-1, keepdims=True)) + EPS) * moe_gain).astype(jnp.bfloat16)
    block_routes = routes.reshape(blocks, TOK_DEV * TOP)
    expert_iota = jnp.arange(EXPERTS, dtype=jnp.int32)
    onehot = (block_routes[:, :, None] == expert_iota[None, None, :]).astype(jnp.int32)
    slots = lax.optimization_barrier(jnp.sum((jnp.cumsum(onehot, axis=1) - 1) * onehot, axis=2))
    block_ids = jnp.broadcast_to(jnp.arange(blocks, dtype=jnp.int32)[:, None], slots.shape)
    row_ids = (slots * blocks + block_ids).reshape(-1).astype(jnp.int32)
    expert_ids = routes.reshape(-1).astype(jnp.int32)
    token_ids = jnp.repeat(jnp.arange(TOKENS, dtype=jnp.int32), TOP)
    holding_arrays = jnp.zeros((EXPERTS, CAP * blocks, D), jnp.bfloat16).at[expert_ids, row_ids].set(moe_in[token_ids])
    gate_all = w_gate.reshape(D, EXPERTS, FF).transpose(1, 0, 2)
    up_all = w_up.reshape(D, EXPERTS, FF).transpose(1, 0, 2)
    down_all = w_down.reshape(EXPERTS, FF, D)

    def one_expert(operands):
        rows_in, gate_w, up_w, down_w = operands
        gate = jnp.dot(rows_in, gate_w, preferred_element_type=jnp.float32)
        upward = jnp.dot(rows_in, up_w, preferred_element_type=jnp.float32)
        inner = (jax.nn.silu(gate) * upward).astype(jnp.bfloat16)
        total = jnp.zeros((rows_in.shape[0], D), jnp.float32)
        for index in range(SLICES):
            part = jnp.dot(inner[:, index * FF_DEV:(index + 1) * FF_DEV], down_w[index * FF_DEV:(index + 1) * FF_DEV], preferred_element_type=jnp.float32)
            total = total + lax.optimization_barrier(part.astype(jnp.bfloat16)).astype(jnp.float32)
        return total
    expert_out = lax.map(one_expert, (holding_arrays, gate_all, up_all, down_all))
    picked = expert_out[expert_ids, row_ids].reshape(TOKENS, TOP, D)
    moe = lax.optimization_barrier(jnp.sum(picked * route_weights[:, :, None], axis=1))
    return (wide + moe).astype(jnp.bfloat16)
```

```python
import jax
import jax.numpy as jnp
from jax import lax
from jax.sharding import PartitionSpec as P

D = 3072
HD = 128
EXPERTS = 8
TOP = 2
CAP = 36


EPS = 1e-06


def swap_heads(x):
    pairs = [(i, lax.axis_size("head") - 1 - i) for i in range(lax.axis_size("head"))]
    return lax.ppermute(x, "head", pairs)


def earlier_sums(own):
    count = lax.axis_size("seq")
    blocks = lax.all_to_all(
        own.reshape(count, own.shape[0] // count, own.shape[1]), "seq", 0, 0, tiled=True
    )
    running = jnp.zeros(blocks.shape[1:], jnp.float32)
    before = []
    for k in range(count):
        before.append(running.astype(jnp.bfloat16))
        running = running + blocks[k].astype(jnp.float32)
    return lax.all_to_all(jnp.stack(before), "seq", 0, 0, tiled=True).reshape(own.shape)


def per_device(
    query,
    keys,
    values,
    resid,
    attn_gain,
    out_weight,
    moe_gain,
    routes,
    route_weights,
    w_gate,
    w_up,
    w_down,
):
    tok_rows = query.shape[0]
    local_heads = query.shape[1] // HD
    seq_count = lax.axis_size("seq")
    head_count = lax.axis_size("head")
    head_pos = lax.axis_index("head")
    half_width = D // head_count
    slices = seq_count * head_count // EXPERTS
    q_three = query.reshape(tok_rows, local_heads, HD)
    k_three = keys.reshape(tok_rows, local_heads, HD)
    value_three_dims = values.reshape(tok_rows, local_heads, HD)
    block_own_state = jnp.einsum(
        "tnd,tne->nde", k_three, value_three_dims, preferred_element_type=jnp.float32
    )
    earlier = earlier_sums(
        block_own_state.astype(jnp.bfloat16).reshape(local_heads * HD, HD)
    ).reshape(local_heads, HD, HD)
    inter = jnp.einsum("tnd,nde->tne", q_three, earlier, preferred_element_type=jnp.float32)
    scores = jnp.einsum("tnd,snd->nts", q_three, k_three, preferred_element_type=jnp.float32)
    causal = jnp.arange(tok_rows)[:, None] >= jnp.arange(tok_rows)[None, :]
    resident_weight_parts = jnp.where(causal, scores, 0.0).astype(jnp.bfloat16)
    inside_block_scores = jnp.einsum(
        "rbj,jrh->brh", resident_weight_parts, value_three_dims, preferred_element_type=jnp.float32
    )
    attention = inter + inside_block_scores
    scale = lax.rsqrt(jnp.mean(attention * attention, axis=-1, keepdims=True) + EPS)
    normed = (
        (attention * scale * attn_gain.reshape(local_heads, HD))
        .astype(jnp.bfloat16)
        .reshape(tok_rows, local_heads * HD)
    )
    everyone = lax.all_gather(normed, "seq", axis=0, tiled=True)
    columns = out_weight.shape[1] // head_count
    projected = jnp.dot(everyone, out_weight, preferred_element_type=jnp.float32)
    kept = lax.dynamic_slice_in_dim(projected, head_pos * columns, columns, 1)
    passed = lax.dynamic_slice_in_dim(projected, (1 - head_pos) * columns, columns, 1)
    mine = (kept + swap_heads(passed.astype(jnp.bfloat16)).astype(jnp.float32)).astype(jnp.bfloat16)
    mine = lax.all_to_all(
        mine.reshape(seq_count, tok_rows, columns), "seq", 0, 0, tiled=True
    )
    other = swap_heads(mine)
    first = jnp.where(head_pos == 0, mine, other)
    second = jnp.where(head_pos == 0, other, mine)
    attended = jnp.stack([first, second], 1).transpose(2, 0, 1, 3).reshape(tok_rows, D)
    resid_other = swap_heads(resid)
    resid_all = jnp.concatenate(
        [
            jnp.where(head_pos == 0, resid, resid_other),
            jnp.where(head_pos == 0, resid_other, resid),
        ],
        axis=1,
    )
    hidden = (attended.astype(jnp.float32) + resid_all.astype(jnp.float32)).astype(jnp.bfloat16)
    wide = hidden.astype(jnp.float32)
    moe_in = (
        wide * lax.rsqrt(jnp.mean(wide * wide, axis=-1, keepdims=True) + EPS) * moe_gain
    ).astype(jnp.bfloat16)
    own_rows = lax.dynamic_slice_in_dim(wide, head_pos * half_width, half_width, 1)
    flat_routes = routes.reshape(-1)
    onehot = (flat_routes[:, None] == jnp.arange(EXPERTS, dtype=jnp.int32)[None, :]).astype(
        jnp.int32
    )
    slots = jnp.sum((jnp.cumsum(onehot, axis=0) - 1) * onehot, axis=1)
    targets = (flat_routes * CAP + slots).reshape(tok_rows, TOP)
    slot_columns = jnp.arange(EXPERTS * CAP, dtype=jnp.int32)
    chosen = (targets[:, :, None] == slot_columns[None, None, :]).astype(jnp.float32)
    picker = jnp.sum(chosen, axis=1).astype(jnp.bfloat16)
    combine_weights = jnp.sum(chosen * route_weights[:, :, None], axis=1)
    contract_rows = (((0,), (0,)), ((), ()))
    own_half = lax.dynamic_slice_in_dim(moe_in, head_pos * half_width, half_width, 1)
    packed = lax.dot_general(
        picker, own_half, contract_rows, preferred_element_type=jnp.float32
    ).astype(jnp.bfloat16)
    chips = slices // head_count
    copies = jnp.broadcast_to(
        packed.reshape(EXPERTS, 1, CAP, half_width), (EXPERTS, chips, CAP, half_width)
    ).reshape(EXPERTS * chips, CAP, half_width)
    received = lax.all_to_all(copies, "seq", 0, 0, tiled=True).reshape(-1, half_width)
    partner = swap_heads(received)
    rows_in = jnp.concatenate(
        [
            jnp.where(head_pos == 0, received, partner),
            jnp.where(head_pos == 0, partner, received),
        ],
        axis=1,
    )
    gate = jnp.dot(rows_in, w_gate, preferred_element_type=jnp.float32)
    upward = jnp.dot(rows_in, w_up, preferred_element_type=jnp.float32)
    inner = (jax.nn.silu(gate) * upward).astype(jnp.bfloat16)
    part = jnp.dot(inner, w_down, preferred_element_type=jnp.float32).astype(jnp.bfloat16)
    kept = lax.dynamic_slice_in_dim(part, head_pos * half_width, half_width, 1)
    passed = lax.dynamic_slice_in_dim(part, (1 - head_pos) * half_width, half_width, 1)
    total = (kept.astype(jnp.float32) + swap_heads(passed).astype(jnp.float32)).astype(jnp.bfloat16)
    back = lax.all_to_all(
        total.reshape(seq_count, CAP, half_width), "seq", 0, 0, tiled=True
    ).reshape(EXPERTS, chips, CAP, half_width)
    high = combine_weights.astype(jnp.bfloat16)
    low = (combine_weights - high.astype(jnp.float32)).astype(jnp.bfloat16)
    moe_out = jnp.zeros((tok_rows, half_width), jnp.float32)
    for chip in range(chips):
        piece = back[:, chip].reshape(EXPERTS * CAP, half_width)
        moe_out = moe_out + jnp.dot(high, piece, preferred_element_type=jnp.float32)
        moe_out = moe_out + jnp.dot(low, piece, preferred_element_type=jnp.float32)
    return (own_rows + moe_out).astype(jnp.bfloat16)


def solution(mesh):
    return jax.shard_map(
        per_device,
        mesh=mesh,
        in_specs=(
            P(("grp", "seq"), "head"),
            P(("grp", "seq"), "head"),
            P(("grp", "seq"), "head"),
            P(("grp", "seq"), "head"),
            P("head"),
            P("head", "seq"),
            P(),
            P(("grp", "seq"), None),
            P(("grp", "seq"), None),
            P(None, ("seq", "head")),
            P(None, ("seq", "head")),
            P(("seq", "head"), None),
        ),
        out_specs=P(("grp", "seq"), "head"),
        check_vma=False,
    )
```

```python
import functools

import jax
import jax.numpy as jnp
from jax import lax
from jax.experimental import pallas as pl
from jax.experimental.pallas import tpu as pltpu
from jax.sharding import PartitionSpec as P

D = 3072
HD = 128
EXPERTS = 8
TOP = 2
CAP = 36


EPS = 1e-06


def swap_heads(x):
    pairs = [(i, lax.axis_size("head") - 1 - i) for i in range(lax.axis_size("head"))]
    return lax.ppermute(x, "head", pairs)


def earlier_sums(own):
    count = lax.axis_size("seq")
    blocks = lax.all_to_all(
        own.reshape(count, own.shape[0] // count, own.shape[1]), "seq", 0, 0, tiled=True
    )
    running = jnp.zeros(blocks.shape[1:], jnp.float32)
    before = []
    for k in range(count):
        before.append(running.astype(jnp.bfloat16))
        running = running + blocks[k].astype(jnp.float32)
    return lax.all_to_all(jnp.stack(before), "seq", 0, 0, tiled=True).reshape(own.shape)


def greet_all(me, count):
    barrier = pltpu.get_barrier_semaphore()

    def greet(step, carry):
        pl.semaphore_signal(
            barrier,
            inc=1,
            device_id={"seq": lax.rem(me + step, count)},
            device_id_type=pl.DeviceIdType.MESH,
        )
        return carry

    lax.fori_loop(1, count, greet, 0)
    pl.semaphore_wait(barrier, count - 1)


def project_kernel(
    count, shard_ref, weight_ref, back_ref, held, made, send_sem, recv_sem, back_send, back_recv, own_sem
):
    me = lax.axis_index("seq")
    outer, inner = me // 2, lax.rem(me, 2)
    outers = count // 2
    partner = outer * 2 + (1 - inner)
    greet_all(me, count)

    def pass_on(source, src, way, to):
        return pltpu.make_async_remote_copy(
            src_ref=src,
            dst_ref=held.at[source],
            send_sem=send_sem.at[source, way],
            recv_sem=recv_sem.at[source],
            device_id={"seq": to},
            device_id_type=pl.DeviceIdType.MESH,
        )

    def go_home(source):
        return pltpu.make_async_remote_copy(
            src_ref=made.at[source],
            dst_ref=back_ref.at[me],
            send_sem=back_send.at[source],
            recv_sem=back_recv.at[me],
            device_id={"seq": source},
            device_id_type=pl.DeviceIdType.MESH,
        )

    def multiply(source, block):
        made[source] = jnp.dot(
            block[...], weight_ref[...], preferred_element_type=jnp.float32
        ).astype(jnp.bfloat16)

    @pl.when(outer + 1 < outers)
    def _():
        pass_on(me, shard_ref, 0, me + 2).start()

    @pl.when(outer > 0)
    def _():
        pass_on(me, shard_ref, 1, me - 2).start()

    pass_on(me, shard_ref, 2, partner).start()
    multiply(me, shard_ref)
    own = pltpu.make_async_copy(made.at[me], back_ref.at[me], own_sem)
    own.start()

    def arrive(source):
        pass_on(source, held.at[source], 2, partner).wait_recv()

    def take(source):
        multiply(source, held.at[source])
        go_home(source).start()

    def step(distance, carry):
        low, high = me - 2 * distance, me + 2 * distance

        @pl.when(outer - distance >= 0)
        def _():
            arrive(low)

            @pl.when(outer + 1 < outers)
            def _():
                pass_on(low, held.at[low], 0, me + 2).start()

            pass_on(low, held.at[low], 2, partner).start()
            take(low)

        @pl.when(outer + distance < outers)
        def _():
            arrive(high)

            @pl.when(outer > 0)
            def _():
                pass_on(high, held.at[high], 1, me - 2).start()

            pass_on(high, held.at[high], 2, partner).start()
            take(high)

        for source in (
            jnp.where(outer - (distance - 1) >= 0, partner - 2 * (distance - 1), -1),
            jnp.where(
                (distance > 1) & (outer + (distance - 1) < outers), partner + 2 * (distance - 1), -1
            ),
        ):

            @pl.when(source >= 0)
            def _():
                arrive(source)
                take(source)

        return carry

    lax.fori_loop(1, outers + 1, step, 0)
    own.wait()

    def finish(step, carry):
        source = lax.rem(me + step, count)
        go_home(source).wait_send()
        pltpu.make_async_remote_copy(
            src_ref=made.at[source],
            dst_ref=back_ref.at[source],
            send_sem=back_send.at[source],
            recv_sem=back_recv.at[source],
            device_id={"seq": source},
            device_id_type=pl.DeviceIdType.MESH,
        ).wait_recv()
        return carry

    lax.fori_loop(1, count, finish, 0)

    def drain(step, carry):
        source = step * 2 + inner

        @pl.when((source <= me) & (outer + 1 < outers))
        def _():
            pass_on(source, held.at[source], 0, me + 2).wait_send()

        @pl.when((source >= me) & (outer > 0))
        def _():
            pass_on(source, held.at[source], 1, me - 2).wait_send()

        pass_on(source, held.at[source], 2, partner).wait_send()
        return carry

    lax.fori_loop(0, outers, drain, 0)


def project(normed, out_weight):
    count = lax.axis_size("seq")
    rows, width = normed.shape
    columns = out_weight.shape[1]
    return pl.pallas_call(
        functools.partial(project_kernel, count),
        name="project",
        out_shape=jax.ShapeDtypeStruct((count, rows, columns), jnp.bfloat16),
        in_specs=[pl.BlockSpec(memory_space=pltpu.VMEM)] * 2,
        out_specs=pl.BlockSpec(memory_space=pltpu.VMEM),
        scratch_shapes=[
            pltpu.VMEM((count, rows, width), jnp.bfloat16),
            pltpu.VMEM((count, rows, columns), jnp.bfloat16),
            pltpu.SemaphoreType.DMA((count, 3)),
            pltpu.SemaphoreType.DMA((count,)),
            pltpu.SemaphoreType.DMA((count,)),
            pltpu.SemaphoreType.DMA((count,)),
            pltpu.SemaphoreType.DMA,
        ],
        compiler_params=pltpu.CompilerParams(
            collective_id=0, has_side_effects=True, vmem_limit_bytes=48 * 1024 * 1024
        ),
    )(normed, out_weight)


def per_device(
    query,
    keys,
    values,
    resid,
    attn_gain,
    out_weight,
    moe_gain,
    routes,
    route_weights,
    w_gate,
    w_up,
    w_down,
):
    tok_rows = query.shape[0]
    local_heads = query.shape[1] // HD
    seq_count = lax.axis_size("seq")
    head_count = lax.axis_size("head")
    head_pos = lax.axis_index("head")
    half_width = D // head_count
    slices = seq_count * head_count // EXPERTS
    q_three = query.reshape(tok_rows, local_heads, HD)
    k_three = keys.reshape(tok_rows, local_heads, HD)
    value_three_dims = values.reshape(tok_rows, local_heads, HD)
    block_own_state = jnp.einsum(
        "tnd,tne->nde", k_three, value_three_dims, preferred_element_type=jnp.float32
    )
    earlier = earlier_sums(
        block_own_state.astype(jnp.bfloat16).reshape(local_heads * HD, HD)
    ).reshape(local_heads, HD, HD)
    inter = jnp.einsum("tnd,nde->tne", q_three, earlier, preferred_element_type=jnp.float32)
    scores = jnp.einsum("tnd,snd->nts", q_three, k_three, preferred_element_type=jnp.float32)
    causal = jnp.arange(tok_rows)[:, None] >= jnp.arange(tok_rows)[None, :]
    resident_weight_parts = jnp.where(causal, scores, 0.0).astype(jnp.bfloat16)
    inside_block_scores = jnp.einsum(
        "rbj,jrh->brh", resident_weight_parts, value_three_dims, preferred_element_type=jnp.float32
    )
    attention = inter + inside_block_scores
    scale = lax.rsqrt(jnp.mean(attention * attention, axis=-1, keepdims=True) + EPS)
    normed = (
        (attention * scale * attn_gain.reshape(local_heads, HD))
        .astype(jnp.bfloat16)
        .reshape(tok_rows, local_heads * HD)
    )
    projected = (
        project(normed, out_weight).transpose(1, 0, 2).reshape(tok_rows, D).astype(jnp.float32)
    )
    placed = lax.dynamic_update_slice_in_dim(
        jnp.zeros((tok_rows, D), jnp.float32), resid.astype(jnp.float32), head_pos * half_width, 1
    )
    half = (projected + placed).astype(jnp.bfloat16)
    other = swap_heads(half)
    hidden = (half.astype(jnp.float32) + other.astype(jnp.float32)).astype(jnp.bfloat16)
    wide = hidden.astype(jnp.float32)
    moe_in = (
        wide * lax.rsqrt(jnp.mean(wide * wide, axis=-1, keepdims=True) + EPS) * moe_gain
    ).astype(jnp.bfloat16)
    own_rows = lax.dynamic_slice_in_dim(wide, head_pos * half_width, half_width, 1)
    flat_routes = routes.reshape(-1)
    onehot = (flat_routes[:, None] == jnp.arange(EXPERTS, dtype=jnp.int32)[None, :]).astype(
        jnp.int32
    )
    slots = jnp.sum((jnp.cumsum(onehot, axis=0) - 1) * onehot, axis=1)
    targets = (flat_routes * CAP + slots).reshape(tok_rows, TOP)
    slot_columns = jnp.arange(EXPERTS * CAP, dtype=jnp.int32)
    chosen = (targets[:, :, None] == slot_columns[None, None, :]).astype(jnp.float32)
    picker = jnp.sum(chosen, axis=1).astype(jnp.bfloat16)
    combine_weights = jnp.sum(chosen * route_weights[:, :, None], axis=1)
    contract_rows = (((0,), (0,)), ((), ()))
    own_half = lax.dynamic_slice_in_dim(moe_in, head_pos * half_width, half_width, 1)
    packed = lax.dot_general(
        picker, own_half, contract_rows, preferred_element_type=jnp.float32
    ).astype(jnp.bfloat16)
    chips = slices // head_count
    copies = jnp.broadcast_to(
        packed.reshape(EXPERTS, 1, CAP, half_width), (EXPERTS, chips, CAP, half_width)
    ).reshape(EXPERTS * chips, CAP, half_width)
    received = lax.all_to_all(copies, "seq", 0, 0, tiled=True).reshape(-1, half_width)
    partner = swap_heads(received)
    rows_in = jnp.concatenate(
        [
            jnp.where(head_pos == 0, received, partner),
            jnp.where(head_pos == 0, partner, received),
        ],
        axis=1,
    )
    gate = jnp.dot(rows_in, w_gate, preferred_element_type=jnp.float32)
    upward = jnp.dot(rows_in, w_up, preferred_element_type=jnp.float32)
    inner = (jax.nn.silu(gate) * upward).astype(jnp.bfloat16)
    part = jnp.dot(inner, w_down, preferred_element_type=jnp.float32).astype(jnp.bfloat16)
    kept = lax.dynamic_slice_in_dim(part, head_pos * half_width, half_width, 1)
    passed = lax.dynamic_slice_in_dim(part, (1 - head_pos) * half_width, half_width, 1)
    total = (kept.astype(jnp.float32) + swap_heads(passed).astype(jnp.float32)).astype(jnp.bfloat16)
    back = lax.all_to_all(
        total.reshape(seq_count, CAP, half_width), "seq", 0, 0, tiled=True
    ).reshape(EXPERTS, chips, CAP, half_width)
    high = combine_weights.astype(jnp.bfloat16)
    low = (combine_weights - high.astype(jnp.float32)).astype(jnp.bfloat16)
    moe_out = jnp.zeros((tok_rows, half_width), jnp.float32)
    for chip in range(chips):
        piece = back[:, chip].reshape(EXPERTS * CAP, half_width)
        moe_out = moe_out + jnp.dot(high, piece, preferred_element_type=jnp.float32)
        moe_out = moe_out + jnp.dot(low, piece, preferred_element_type=jnp.float32)
    return (own_rows + moe_out).astype(jnp.bfloat16)


def solution(mesh):
    return jax.shard_map(
        per_device,
        mesh=mesh,
        in_specs=(
            P(("grp", "seq"), "head"),
            P(("grp", "seq"), "head"),
            P(("grp", "seq"), "head"),
            P(("grp", "seq"), "head"),
            P("head"),
            P("head", "seq"),
            P(),
            P(("grp", "seq"), None),
            P(("grp", "seq"), None),
            P(None, ("seq", "head")),
            P(None, ("seq", "head")),
            P(("seq", "head"), None),
        ),
        out_specs=P(("grp", "seq"), "head"),
        check_vma=False,
    )
```

```python
import functools

import jax
import jax.numpy as jnp
from jax import lax
from jax.experimental import pallas as pl
from jax.experimental.pallas import tpu as pltpu
from jax.sharding import PartitionSpec as P

D = 3072
HD = 128
EXPERTS = 8
TOP = 2
CAP = 36


EPS = 1e-06


def swap_heads(x):
    pairs = [(i, lax.axis_size("head") - 1 - i) for i in range(lax.axis_size("head"))]
    return lax.ppermute(x, "head", pairs)


def greet_all(me, count, pair=False):
    barrier = pltpu.get_barrier_semaphore()

    def greet(step, carry):
        pl.semaphore_signal(
            barrier,
            inc=1,
            device_id={"seq": lax.rem(me + step, count)},
            device_id_type=pl.DeviceIdType.MESH,
        )
        return carry

    lax.fori_loop(1, count, greet, 0)
    if pair:
        pl.semaphore_signal(
            barrier,
            inc=1,
            device_id={"head": 1 - lax.axis_index("head")},
            device_id_type=pl.DeviceIdType.MESH,
        )
    pl.semaphore_wait(barrier, count - 1 + int(pair))


def send_to(src, dst, send_sem, recv_sem, **device):
    return pltpu.make_async_remote_copy(
        src_ref=src,
        dst_ref=dst,
        send_sem=send_sem,
        recv_sem=recv_sem,
        device_id=device,
        device_id_type=pl.DeviceIdType.MESH,
    )


def sums_kernel(count, own_ref, out_ref, got, made, send_sem, recv_sem, home_send, home_recv):
    me = lax.axis_index("seq")
    greet_all(me, count)

    def out(other):
        return send_to(
            own_ref.at[other], got.at[me], send_sem.at[other], recv_sem.at[me], seq=other
        )

    def arrival(other):
        return send_to(
            own_ref.at[other], got.at[other], send_sem.at[other], recv_sem.at[other], seq=other
        )

    def home(other):
        return send_to(
            made.at[other], out_ref.at[me], home_send.at[other], home_recv.at[me], seq=other
        )

    def home_arrival(other):
        return send_to(
            made.at[other], out_ref.at[other], home_send.at[other], home_recv.at[other], seq=other
        )

    def start(step, carry):
        out(lax.rem(me + step, count)).start()
        return carry

    lax.fori_loop(1, count, start, 0)
    got[me] = own_ref[me]

    def add(block, running):
        made[block] = running.astype(jnp.bfloat16)

        @pl.when(block != me)
        def _():
            arrival(block).wait_recv()
            home(block).start()

        return running + got[block].astype(jnp.float32)

    lax.fori_loop(0, count, add, jnp.zeros(got.shape[1:], jnp.float32))
    out_ref[me] = made[me]

    def finish(step, carry):
        other = lax.rem(me + step, count)
        out(other).wait_send()
        home_arrival(other).wait_recv()
        home(other).wait_send()
        return carry

    lax.fori_loop(1, count, finish, 0)


def earlier_sums(own):
    count = lax.axis_size("seq")
    shape = (count, own.shape[0] // count, own.shape[1])
    return pl.pallas_call(
        functools.partial(sums_kernel, count),
        name="sums",
        out_shape=jax.ShapeDtypeStruct(shape, jnp.bfloat16),
        in_specs=[pl.BlockSpec(memory_space=pltpu.VMEM)],
        out_specs=pl.BlockSpec(memory_space=pltpu.VMEM),
        scratch_shapes=[pltpu.VMEM(shape, jnp.bfloat16)] * 2
        + [pltpu.SemaphoreType.DMA((count,))] * 4,
        compiler_params=pltpu.CompilerParams(
            collective_id=1, has_side_effects=True, vmem_limit_bytes=16 * 1024 * 1024
        ),
    )(own.reshape(shape)).reshape(own.shape)


def dispatch_kernel(
    count, packed_ref, rows_ref, send_sem, recv_sem, pair_send, pair_recv, own_sem
):
    me, head = lax.axis_index("seq"), lax.axis_index("head")
    half = packed_ref.shape[2]
    greet_all(me, count, True)

    def place(source, side):
        return rows_ref.at[source, :, pl.ds(pl.multiple_of(side * half, 128), half)]

    def out(other):
        return send_to(
            packed_ref.at[other], place(me, head), send_sem.at[other], recv_sem.at[me], seq=other
        )

    def arrival(other):
        return send_to(
            packed_ref.at[other],
            place(other, head),
            send_sem.at[other],
            recv_sem.at[other],
            seq=other,
        )

    def pair(source, src, side):
        return send_to(
            src, place(source, side), pair_send.at[source], pair_recv.at[source], head=1 - head
        )

    def start(step, carry):
        out(lax.rem(me + step, count)).start()
        return carry

    lax.fori_loop(1, count, start, 0)
    own = pltpu.make_async_copy(packed_ref.at[me], place(me, head), own_sem)
    own.start()
    pair(me, packed_ref.at[me], head).start()

    def hand_on(step, carry):
        source = lax.rem(me - step + count, count)
        arrival(source).wait_recv()
        pair(source, place(source, head), head).start()
        return carry

    lax.fori_loop(1, count, hand_on, 0)
    own.wait()

    def finish(source, carry):
        pair(source, place(source, head), head).wait_send()
        pair(source, place(source, 1 - head), 1 - head).wait_recv()

        @pl.when(source != me)
        def _():
            out(source).wait_send()

        return carry

    lax.fori_loop(0, count, finish, 0)


def dispatch(packed):
    count, slots, half = packed.shape
    return pl.pallas_call(
        functools.partial(dispatch_kernel, count),
        name="dispatch",
        out_shape=jax.ShapeDtypeStruct((count, slots, 2 * half), jnp.bfloat16),
        in_specs=[pl.BlockSpec(memory_space=pltpu.VMEM)],
        out_specs=pl.BlockSpec(memory_space=pltpu.VMEM),
        scratch_shapes=[pltpu.SemaphoreType.DMA((count,))] * 4 + [pltpu.SemaphoreType.DMA],
        compiler_params=pltpu.CompilerParams(
            collective_id=2, has_side_effects=True, vmem_limit_bytes=32 * 1024 * 1024
        ),
    )(packed)


def combine_kernel(
    count, part_ref, back_ref, theirs, total, send_sem, recv_sem, pair_send, pair_recv
):
    me, head = lax.axis_index("seq"), lax.axis_index("head")
    half = back_ref.shape[2]
    greet_all(me, count, True)

    def pair(block):
        columns = pl.ds(pl.multiple_of((1 - head) * half, 128), half)
        return send_to(
            part_ref.at[block, :, columns],
            theirs.at[block],
            pair_send.at[block],
            pair_recv.at[block],
            head=1 - head,
        )

    def home(other):
        return send_to(
            total.at[other], back_ref.at[me], send_sem.at[other], recv_sem.at[me], seq=other
        )

    def home_arrival(other):
        return send_to(
            total.at[other], back_ref.at[other], send_sem.at[other], recv_sem.at[other], seq=other
        )

    def start(step, carry):
        pair(lax.rem(me + step, count)).start()
        return carry

    lax.fori_loop(1, count + 1, start, 0)
    kept = pl.ds(pl.multiple_of(head * half, 128), half)

    def add(step, carry):
        block = lax.rem(me + step, count)
        pair(block).wait_recv()
        total[block] = (
            part_ref[block, :, kept].astype(jnp.float32) + theirs[block].astype(jnp.float32)
        ).astype(jnp.bfloat16)

        @pl.when(block != me)
        def _():
            home(block).start()

        return carry

    lax.fori_loop(1, count + 1, add, 0)
    back_ref[me] = total[me]

    def finish(block, carry):
        pair(block).wait_send()

        @pl.when(block != me)
        def _():
            home_arrival(block).wait_recv()
            home(block).wait_send()

        return carry

    lax.fori_loop(0, count, finish, 0)


def combine(part):
    count, slots, width = part.shape
    shape = (count, slots, width // 2)
    return pl.pallas_call(
        functools.partial(combine_kernel, count),
        name="combine",
        out_shape=jax.ShapeDtypeStruct(shape, jnp.bfloat16),
        in_specs=[pl.BlockSpec(memory_space=pltpu.VMEM)],
        out_specs=pl.BlockSpec(memory_space=pltpu.VMEM),
        scratch_shapes=[pltpu.VMEM(shape, jnp.bfloat16)] * 2
        + [pltpu.SemaphoreType.DMA((count,))] * 4,
        compiler_params=pltpu.CompilerParams(
            collective_id=3, has_side_effects=True, vmem_limit_bytes=40 * 1024 * 1024
        ),
    )(part)


def project_kernel(
    count, shard_ref, weight_ref, back_ref, held, made, send_sem, recv_sem, back_send, back_recv, own_sem
):
    me = lax.axis_index("seq")
    outer, inner = me // 2, lax.rem(me, 2)
    outers = count // 2
    partner = outer * 2 + (1 - inner)
    greet_all(me, count)

    def pass_on(source, src, way, to):
        return pltpu.make_async_remote_copy(
            src_ref=src,
            dst_ref=held.at[source],
            send_sem=send_sem.at[source, way],
            recv_sem=recv_sem.at[source],
            device_id={"seq": to},
            device_id_type=pl.DeviceIdType.MESH,
        )

    def go_home(source):
        return pltpu.make_async_remote_copy(
            src_ref=made.at[source],
            dst_ref=back_ref.at[me],
            send_sem=back_send.at[source],
            recv_sem=back_recv.at[me],
            device_id={"seq": source},
            device_id_type=pl.DeviceIdType.MESH,
        )

    def multiply(source, block):
        made[source] = jnp.dot(
            block[...], weight_ref[...], preferred_element_type=jnp.float32
        ).astype(jnp.bfloat16)

    @pl.when(outer + 1 < outers)
    def _():
        pass_on(me, shard_ref, 0, me + 2).start()

    @pl.when(outer > 0)
    def _():
        pass_on(me, shard_ref, 1, me - 2).start()

    pass_on(me, shard_ref, 2, partner).start()
    multiply(me, shard_ref)
    own = pltpu.make_async_copy(made.at[me], back_ref.at[me], own_sem)
    own.start()

    def arrive(source):
        pass_on(source, held.at[source], 2, partner).wait_recv()

    def take(source):
        multiply(source, held.at[source])
        go_home(source).start()

    def step(distance, carry):
        low, high = me - 2 * distance, me + 2 * distance

        @pl.when(outer - distance >= 0)
        def _():
            arrive(low)

            @pl.when(outer + 1 < outers)
            def _():
                pass_on(low, held.at[low], 0, me + 2).start()

            pass_on(low, held.at[low], 2, partner).start()
            take(low)

        @pl.when(outer + distance < outers)
        def _():
            arrive(high)

            @pl.when(outer > 0)
            def _():
                pass_on(high, held.at[high], 1, me - 2).start()

            pass_on(high, held.at[high], 2, partner).start()
            take(high)

        for source in (
            jnp.where(outer - (distance - 1) >= 0, partner - 2 * (distance - 1), -1),
            jnp.where(
                (distance > 1) & (outer + (distance - 1) < outers), partner + 2 * (distance - 1), -1
            ),
        ):

            @pl.when(source >= 0)
            def _():
                arrive(source)
                take(source)

        return carry

    lax.fori_loop(1, outers + 1, step, 0)
    own.wait()

    def finish(step, carry):
        source = lax.rem(me + step, count)
        go_home(source).wait_send()
        pltpu.make_async_remote_copy(
            src_ref=made.at[source],
            dst_ref=back_ref.at[source],
            send_sem=back_send.at[source],
            recv_sem=back_recv.at[source],
            device_id={"seq": source},
            device_id_type=pl.DeviceIdType.MESH,
        ).wait_recv()
        return carry

    lax.fori_loop(1, count, finish, 0)

    def drain(step, carry):
        source = step * 2 + inner

        @pl.when((source <= me) & (outer + 1 < outers))
        def _():
            pass_on(source, held.at[source], 0, me + 2).wait_send()

        @pl.when((source >= me) & (outer > 0))
        def _():
            pass_on(source, held.at[source], 1, me - 2).wait_send()

        pass_on(source, held.at[source], 2, partner).wait_send()
        return carry

    lax.fori_loop(0, outers, drain, 0)


def project(normed, out_weight):
    count = lax.axis_size("seq")
    rows, width = normed.shape
    columns = out_weight.shape[1]
    return pl.pallas_call(
        functools.partial(project_kernel, count),
        name="project",
        out_shape=jax.ShapeDtypeStruct((count, rows, columns), jnp.bfloat16),
        in_specs=[pl.BlockSpec(memory_space=pltpu.VMEM)] * 2,
        out_specs=pl.BlockSpec(memory_space=pltpu.VMEM),
        scratch_shapes=[
            pltpu.VMEM((count, rows, width), jnp.bfloat16),
            pltpu.VMEM((count, rows, columns), jnp.bfloat16),
            pltpu.SemaphoreType.DMA((count, 3)),
            pltpu.SemaphoreType.DMA((count,)),
            pltpu.SemaphoreType.DMA((count,)),
            pltpu.SemaphoreType.DMA((count,)),
            pltpu.SemaphoreType.DMA,
        ],
        compiler_params=pltpu.CompilerParams(
            collective_id=0, has_side_effects=True, vmem_limit_bytes=48 * 1024 * 1024
        ),
    )(normed, out_weight)


def per_device(
    query,
    keys,
    values,
    resid,
    attn_gain,
    out_weight,
    moe_gain,
    routes,
    route_weights,
    w_gate,
    w_up,
    w_down,
):
    tok_rows = query.shape[0]
    local_heads = query.shape[1] // HD
    seq_count = lax.axis_size("seq")
    head_count = lax.axis_size("head")
    head_pos = lax.axis_index("head")
    half_width = D // head_count
    slices = seq_count * head_count // EXPERTS
    q_three = query.reshape(tok_rows, local_heads, HD)
    k_three = keys.reshape(tok_rows, local_heads, HD)
    value_three_dims = values.reshape(tok_rows, local_heads, HD)
    block_own_state = jnp.einsum(
        "tnd,tne->nde", k_three, value_three_dims, preferred_element_type=jnp.float32
    )
    earlier = earlier_sums(
        block_own_state.astype(jnp.bfloat16).reshape(local_heads * HD, HD)
    ).reshape(local_heads, HD, HD)
    inter = jnp.einsum("tnd,nde->tne", q_three, earlier, preferred_element_type=jnp.float32)
    scores = jnp.einsum("tnd,snd->nts", q_three, k_three, preferred_element_type=jnp.float32)
    causal = jnp.arange(tok_rows)[:, None] >= jnp.arange(tok_rows)[None, :]
    resident_weight_parts = jnp.where(causal, scores, 0.0).astype(jnp.bfloat16)
    inside_block_scores = jnp.einsum(
        "rbj,jrh->brh", resident_weight_parts, value_three_dims, preferred_element_type=jnp.float32
    )
    attention = inter + inside_block_scores
    scale = lax.rsqrt(jnp.mean(attention * attention, axis=-1, keepdims=True) + EPS)
    normed = (
        (attention * scale * attn_gain.reshape(local_heads, HD))
        .astype(jnp.bfloat16)
        .reshape(tok_rows, local_heads * HD)
    )
    projected = (
        project(normed, out_weight).transpose(1, 0, 2).reshape(tok_rows, D).astype(jnp.float32)
    )
    placed = lax.dynamic_update_slice_in_dim(
        jnp.zeros((tok_rows, D), jnp.float32), resid.astype(jnp.float32), head_pos * half_width, 1
    )
    half = (projected + placed).astype(jnp.bfloat16)
    other = swap_heads(half)
    hidden = (half.astype(jnp.float32) + other.astype(jnp.float32)).astype(jnp.bfloat16)
    wide = hidden.astype(jnp.float32)
    moe_in = (
        wide * lax.rsqrt(jnp.mean(wide * wide, axis=-1, keepdims=True) + EPS) * moe_gain
    ).astype(jnp.bfloat16)
    own_rows = lax.dynamic_slice_in_dim(wide, head_pos * half_width, half_width, 1)
    flat_routes = routes.reshape(-1)
    onehot = (flat_routes[:, None] == jnp.arange(EXPERTS, dtype=jnp.int32)[None, :]).astype(
        jnp.int32
    )
    slots = jnp.sum((jnp.cumsum(onehot, axis=0) - 1) * onehot, axis=1)
    targets = (flat_routes * CAP + slots).reshape(tok_rows, TOP)
    slot_columns = jnp.arange(EXPERTS * CAP, dtype=jnp.int32)
    chosen = (targets[:, :, None] == slot_columns[None, None, :]).astype(jnp.float32)
    picker = jnp.sum(chosen, axis=1).astype(jnp.bfloat16)
    combine_weights = jnp.sum(chosen * route_weights[:, :, None], axis=1)
    contract_rows = (((0,), (0,)), ((), ()))
    own_half = lax.dynamic_slice_in_dim(moe_in, head_pos * half_width, half_width, 1)
    packed = lax.dot_general(
        picker, own_half, contract_rows, preferred_element_type=jnp.float32
    ).astype(jnp.bfloat16)
    chips = slices // head_count
    copies = jnp.broadcast_to(
        packed.reshape(EXPERTS, 1, CAP, half_width), (EXPERTS, chips, CAP, half_width)
    ).reshape(EXPERTS * chips, CAP, half_width)
    rows_in = dispatch(copies).reshape(-1, D)
    gate = jnp.dot(rows_in, w_gate, preferred_element_type=jnp.float32)
    upward = jnp.dot(rows_in, w_up, preferred_element_type=jnp.float32)
    inner = (jax.nn.silu(gate) * upward).astype(jnp.bfloat16)
    part = jnp.dot(inner, w_down, preferred_element_type=jnp.float32).astype(jnp.bfloat16)
    back = combine(part.reshape(seq_count, CAP, D)).reshape(EXPERTS, chips, CAP, half_width)
    high = combine_weights.astype(jnp.bfloat16)
    low = (combine_weights - high.astype(jnp.float32)).astype(jnp.bfloat16)
    moe_out = jnp.zeros((tok_rows, half_width), jnp.float32)
    for chip in range(chips):
        piece = back[:, chip].reshape(EXPERTS * CAP, half_width)
        moe_out = moe_out + jnp.dot(high, piece, preferred_element_type=jnp.float32)
        moe_out = moe_out + jnp.dot(low, piece, preferred_element_type=jnp.float32)
    return (own_rows + moe_out).astype(jnp.bfloat16)


def solution(mesh):
    return jax.shard_map(
        per_device,
        mesh=mesh,
        in_specs=(
            P(("grp", "seq"), "head"),
            P(("grp", "seq"), "head"),
            P(("grp", "seq"), "head"),
            P(("grp", "seq"), "head"),
            P("head"),
            P("head", "seq"),
            P(),
            P(("grp", "seq"), None),
            P(("grp", "seq"), None),
            P(None, ("seq", "head")),
            P(None, ("seq", "head")),
            P(("seq", "head"), None),
        ),
        out_specs=P(("grp", "seq"), "head"),
        check_vma=False,
    )
```

```python
import functools

import jax
import jax.numpy as jnp
from jax import lax
from jax.experimental import pallas as pl
from jax.experimental.pallas import tpu as pltpu
from jax.sharding import PartitionSpec as P

D = 3072
HD = 128
EXPERTS = 8
TOP = 2
CAP = 36


EPS = 1e-06


def swap_heads(x):
    pairs = [(i, lax.axis_size("head") - 1 - i) for i in range(lax.axis_size("head"))]
    return lax.ppermute(x, "head", pairs)


def greet_all(me, count, pair=False):
    barrier = pltpu.get_barrier_semaphore()

    def greet(step, carry):
        pl.semaphore_signal(
            barrier,
            inc=1,
            device_id={"seq": lax.rem(me + step, count)},
            device_id_type=pl.DeviceIdType.MESH,
        )
        return carry

    lax.fori_loop(1, count, greet, 0)
    if pair:
        pl.semaphore_signal(
            barrier,
            inc=1,
            device_id={"head": 1 - lax.axis_index("head")},
            device_id_type=pl.DeviceIdType.MESH,
        )
    pl.semaphore_wait(barrier, count - 1 + int(pair))


def grant(*blocks):
    total = 1 << 20
    for shape in blocks:
        cells = (-(-shape[-1] // 128) * 128) * (-(-shape[-2] // 16) * 16)
        for size in shape[:-2]:
            cells = cells * size
        total = total + 2 * cells
    return total


def send_to(src, dst, send_sem, recv_sem, **device):
    return pltpu.make_async_remote_copy(
        src_ref=src,
        dst_ref=dst,
        send_sem=send_sem,
        recv_sem=recv_sem,
        device_id=device,
        device_id_type=pl.DeviceIdType.MESH,
    )


def sums_kernel(count, own_ref, out_ref, got, made, send_sem, recv_sem, home_send, home_recv):
    me = lax.axis_index("seq")
    greet_all(me, count)

    def out(other):
        return send_to(
            own_ref.at[other], got.at[me], send_sem.at[other], recv_sem.at[me], seq=other
        )

    def arrival(other):
        return send_to(
            own_ref.at[other], got.at[other], send_sem.at[other], recv_sem.at[other], seq=other
        )

    def home(other):
        return send_to(
            made.at[other], out_ref.at[me], home_send.at[other], home_recv.at[me], seq=other
        )

    def home_arrival(other):
        return send_to(
            made.at[other], out_ref.at[other], home_send.at[other], home_recv.at[other], seq=other
        )

    def start(step, carry):
        out(lax.rem(me + step, count)).start()
        return carry

    lax.fori_loop(1, count, start, 0)
    got[me] = own_ref[me]

    def add(block, running):
        made[block] = running.astype(jnp.bfloat16)

        @pl.when(block != me)
        def _():
            arrival(block).wait_recv()
            home(block).start()

        return running + got[block].astype(jnp.float32)

    lax.fori_loop(0, count, add, jnp.zeros(got.shape[1:], jnp.float32))
    out_ref[me] = made[me]

    def finish(step, carry):
        other = lax.rem(me + step, count)
        out(other).wait_send()
        home_arrival(other).wait_recv()
        home(other).wait_send()
        return carry

    lax.fori_loop(1, count, finish, 0)


def earlier_sums(own):
    count = lax.axis_size("seq")
    shape = (count, own.shape[0] // count, own.shape[1])
    return pl.pallas_call(
        functools.partial(sums_kernel, count),
        name="sums",
        out_shape=jax.ShapeDtypeStruct(shape, jnp.bfloat16),
        in_specs=[pl.BlockSpec(memory_space=pltpu.VMEM)],
        out_specs=pl.BlockSpec(memory_space=pltpu.VMEM),
        scratch_shapes=[pltpu.VMEM(shape, jnp.bfloat16)] * 2
        + [pltpu.SemaphoreType.DMA((count,))] * 4,
        compiler_params=pltpu.CompilerParams(
            collective_id=1, has_side_effects=True, vmem_limit_bytes=grant(shape, shape, shape, shape, shape)
        ),
    )(own.reshape(shape)).reshape(own.shape)


def dispatch_kernel(
    count, packed_ref, rows_ref, send_sem, recv_sem, pair_send, pair_recv, own_sem
):
    me, head = lax.axis_index("seq"), lax.axis_index("head")
    half = packed_ref.shape[2]
    greet_all(me, count, True)

    def place(source, side):
        return rows_ref.at[source, :, pl.ds(pl.multiple_of(side * half, 128), half)]

    def out(other):
        return send_to(
            packed_ref.at[other], place(me, head), send_sem.at[other], recv_sem.at[me], seq=other
        )

    def arrival(other):
        return send_to(
            packed_ref.at[other],
            place(other, head),
            send_sem.at[other],
            recv_sem.at[other],
            seq=other,
        )

    def pair(source, src, side):
        return send_to(
            src, place(source, side), pair_send.at[source], pair_recv.at[source], head=1 - head
        )

    def start(step, carry):
        out(lax.rem(me + step, count)).start()
        return carry

    lax.fori_loop(1, count, start, 0)
    own = pltpu.make_async_copy(packed_ref.at[me], place(me, head), own_sem)
    own.start()
    pair(me, packed_ref.at[me], head).start()

    def hand_on(step, carry):
        source = lax.rem(me - step + count, count)
        arrival(source).wait_recv()
        pair(source, place(source, head), head).start()
        return carry

    lax.fori_loop(1, count, hand_on, 0)
    own.wait()

    def finish(source, carry):
        pair(source, place(source, head), head).wait_send()
        pair(source, place(source, 1 - head), 1 - head).wait_recv()

        @pl.when(source != me)
        def _():
            out(source).wait_send()

        return carry

    lax.fori_loop(0, count, finish, 0)


def dispatch(packed):
    count, slots, half = packed.shape
    return pl.pallas_call(
        functools.partial(dispatch_kernel, count),
        name="dispatch",
        out_shape=jax.ShapeDtypeStruct((count, slots, 2 * half), jnp.bfloat16),
        in_specs=[pl.BlockSpec(memory_space=pltpu.VMEM)],
        out_specs=pl.BlockSpec(memory_space=pltpu.VMEM),
        scratch_shapes=[pltpu.SemaphoreType.DMA((count,))] * 4 + [pltpu.SemaphoreType.DMA],
        compiler_params=pltpu.CompilerParams(
            collective_id=2, has_side_effects=True, vmem_limit_bytes=grant((count, slots, 3 * half))
        ),
    )(packed)


def combine_kernel(
    count, part_ref, back_ref, theirs, total, send_sem, recv_sem, pair_send, pair_recv
):
    me, head = lax.axis_index("seq"), lax.axis_index("head")
    half = back_ref.shape[2]
    greet_all(me, count, True)

    def pair(block):
        columns = pl.ds(pl.multiple_of((1 - head) * half, 128), half)
        return send_to(
            part_ref.at[block, :, columns],
            theirs.at[block],
            pair_send.at[block],
            pair_recv.at[block],
            head=1 - head,
        )

    def home(other):
        return send_to(
            total.at[other], back_ref.at[me], send_sem.at[other], recv_sem.at[me], seq=other
        )

    def home_arrival(other):
        return send_to(
            total.at[other], back_ref.at[other], send_sem.at[other], recv_sem.at[other], seq=other
        )

    def start(step, carry):
        pair(lax.rem(me + step, count)).start()
        return carry

    lax.fori_loop(1, count + 1, start, 0)
    kept = pl.ds(pl.multiple_of(head * half, 128), half)

    def add(step, carry):
        block = lax.rem(me + step, count)
        pair(block).wait_recv()
        total[block] = (
            part_ref[block, :, kept].astype(jnp.float32) + theirs[block].astype(jnp.float32)
        ).astype(jnp.bfloat16)

        @pl.when(block != me)
        def _():
            home(block).start()

        return carry

    lax.fori_loop(1, count + 1, add, 0)
    back_ref[me] = total[me]

    def finish(block, carry):
        pair(block).wait_send()

        @pl.when(block != me)
        def _():
            home_arrival(block).wait_recv()
            home(block).wait_send()

        return carry

    lax.fori_loop(0, count, finish, 0)


def combine(part):
    count, slots, width = part.shape
    shape = (count, slots, width // 2)
    return pl.pallas_call(
        functools.partial(combine_kernel, count),
        name="combine",
        out_shape=jax.ShapeDtypeStruct(shape, jnp.bfloat16),
        in_specs=[pl.BlockSpec(memory_space=pltpu.VMEM)],
        out_specs=pl.BlockSpec(memory_space=pltpu.VMEM),
        scratch_shapes=[pltpu.VMEM(shape, jnp.bfloat16)] * 2
        + [pltpu.SemaphoreType.DMA((count,))] * 4,
        compiler_params=pltpu.CompilerParams(
            collective_id=3, has_side_effects=True, vmem_limit_bytes=grant(shape, shape, shape, part.shape, shape[1:])
        ),
    )(part)


def project_kernel(
    count, shard_ref, weight_ref, back_ref, held, made, send_sem, recv_sem, back_send, back_recv, own_sem
):
    me = lax.axis_index("seq")
    outer, inner = me // 2, lax.rem(me, 2)
    outers = count // 2
    partner = outer * 2 + (1 - inner)
    greet_all(me, count)

    def pass_on(source, src, way, to):
        return pltpu.make_async_remote_copy(
            src_ref=src,
            dst_ref=held.at[source],
            send_sem=send_sem.at[source, way],
            recv_sem=recv_sem.at[source],
            device_id={"seq": to},
            device_id_type=pl.DeviceIdType.MESH,
        )

    def go_home(source):
        return pltpu.make_async_remote_copy(
            src_ref=made.at[source],
            dst_ref=back_ref.at[me],
            send_sem=back_send.at[source],
            recv_sem=back_recv.at[me],
            device_id={"seq": source},
            device_id_type=pl.DeviceIdType.MESH,
        )

    def multiply(source, block):
        made[source] = jnp.dot(
            block[...], weight_ref[...], preferred_element_type=jnp.float32
        ).astype(jnp.bfloat16)

    @pl.when(outer + 1 < outers)
    def _():
        pass_on(me, shard_ref, 0, me + 2).start()

    @pl.when(outer > 0)
    def _():
        pass_on(me, shard_ref, 1, me - 2).start()

    pass_on(me, shard_ref, 2, partner).start()
    multiply(me, shard_ref)
    own = pltpu.make_async_copy(made.at[me], back_ref.at[me], own_sem)
    own.start()

    def arrive(source):
        pass_on(source, held.at[source], 2, partner).wait_recv()

    def take(source):
        multiply(source, held.at[source])
        go_home(source).start()

    def step(distance, carry):
        low, high = me - 2 * distance, me + 2 * distance

        @pl.when(outer - distance >= 0)
        def _():
            arrive(low)

            @pl.when(outer + 1 < outers)
            def _():
                pass_on(low, held.at[low], 0, me + 2).start()

            pass_on(low, held.at[low], 2, partner).start()
            take(low)

        @pl.when(outer + distance < outers)
        def _():
            arrive(high)

            @pl.when(outer > 0)
            def _():
                pass_on(high, held.at[high], 1, me - 2).start()

            pass_on(high, held.at[high], 2, partner).start()
            take(high)

        for source in (
            jnp.where(outer - (distance - 1) >= 0, partner - 2 * (distance - 1), -1),
            jnp.where(
                (distance > 1) & (outer + (distance - 1) < outers), partner + 2 * (distance - 1), -1
            ),
        ):

            @pl.when(source >= 0)
            def _():
                arrive(source)
                take(source)

        return carry

    lax.fori_loop(1, outers + 1, step, 0)
    own.wait()

    def finish(step, carry):
        source = lax.rem(me + step, count)
        go_home(source).wait_send()
        pltpu.make_async_remote_copy(
            src_ref=made.at[source],
            dst_ref=back_ref.at[source],
            send_sem=back_send.at[source],
            recv_sem=back_recv.at[source],
            device_id={"seq": source},
            device_id_type=pl.DeviceIdType.MESH,
        ).wait_recv()
        return carry

    lax.fori_loop(1, count, finish, 0)

    def drain(step, carry):
        source = step * 2 + inner

        @pl.when((source <= me) & (outer + 1 < outers))
        def _():
            pass_on(source, held.at[source], 0, me + 2).wait_send()

        @pl.when((source >= me) & (outer > 0))
        def _():
            pass_on(source, held.at[source], 1, me - 2).wait_send()

        pass_on(source, held.at[source], 2, partner).wait_send()
        return carry

    lax.fori_loop(0, outers, drain, 0)


def project(normed, out_weight):
    count = lax.axis_size("seq")
    rows, width = normed.shape
    columns = out_weight.shape[1]
    return pl.pallas_call(
        functools.partial(project_kernel, count),
        name="project",
        out_shape=jax.ShapeDtypeStruct((count, rows, columns), jnp.bfloat16),
        in_specs=[pl.BlockSpec(memory_space=pltpu.VMEM)] * 2,
        out_specs=pl.BlockSpec(memory_space=pltpu.VMEM),
        scratch_shapes=[
            pltpu.VMEM((count, rows, width), jnp.bfloat16),
            pltpu.VMEM((count, rows, columns), jnp.bfloat16),
            pltpu.SemaphoreType.DMA((count, 3)),
            pltpu.SemaphoreType.DMA((count,)),
            pltpu.SemaphoreType.DMA((count,)),
            pltpu.SemaphoreType.DMA((count,)),
            pltpu.SemaphoreType.DMA,
        ],
        compiler_params=pltpu.CompilerParams(
            collective_id=0,
            has_side_effects=True,
            vmem_limit_bytes=grant(
                (count + 1, rows, width), (2 * count + 8, rows, columns), out_weight.shape
            ),
        ),
    )(normed, out_weight)


def per_device(
    query,
    keys,
    values,
    resid,
    attn_gain,
    out_weight,
    moe_gain,
    routes,
    route_weights,
    w_gate,
    w_up,
    w_down,
):
    tok_rows = query.shape[0]
    local_heads = query.shape[1] // HD
    seq_count = lax.axis_size("seq")
    head_count = lax.axis_size("head")
    head_pos = lax.axis_index("head")
    half_width = D // head_count
    slices = seq_count * head_count // EXPERTS
    q_three = query.reshape(tok_rows, local_heads, HD)
    k_three = keys.reshape(tok_rows, local_heads, HD)
    value_three_dims = values.reshape(tok_rows, local_heads, HD)
    block_own_state = jnp.einsum(
        "tnd,tne->nde", k_three, value_three_dims, preferred_element_type=jnp.float32
    )
    earlier = earlier_sums(
        block_own_state.astype(jnp.bfloat16).reshape(local_heads * HD, HD)
    ).reshape(local_heads, HD, HD)
    inter = jnp.einsum("tnd,nde->tne", q_three, earlier, preferred_element_type=jnp.float32)
    scores = jnp.einsum("tnd,snd->nts", q_three, k_three, preferred_element_type=jnp.float32)
    causal = jnp.arange(tok_rows)[:, None] >= jnp.arange(tok_rows)[None, :]
    resident_weight_parts = jnp.where(causal, scores, 0.0).astype(jnp.bfloat16)
    inside_block_scores = jnp.einsum(
        "rbj,jrh->brh", resident_weight_parts, value_three_dims, preferred_element_type=jnp.float32
    )
    attention = inter + inside_block_scores
    scale = lax.rsqrt(jnp.mean(attention * attention, axis=-1, keepdims=True) + EPS)
    normed = (
        (attention * scale * attn_gain.reshape(local_heads, HD))
        .astype(jnp.bfloat16)
        .reshape(tok_rows, local_heads * HD)
    )
    projected = (
        project(normed, out_weight).transpose(1, 0, 2).reshape(tok_rows, D).astype(jnp.float32)
    )
    placed = lax.dynamic_update_slice_in_dim(
        jnp.zeros((tok_rows, D), jnp.float32), resid.astype(jnp.float32), head_pos * half_width, 1
    )
    half = (projected + placed).astype(jnp.bfloat16)
    other = swap_heads(half)
    hidden = (half.astype(jnp.float32) + other.astype(jnp.float32)).astype(jnp.bfloat16)
    wide = hidden.astype(jnp.float32)
    moe_in = (
        wide * lax.rsqrt(jnp.mean(wide * wide, axis=-1, keepdims=True) + EPS) * moe_gain
    ).astype(jnp.bfloat16)
    own_rows = lax.dynamic_slice_in_dim(wide, head_pos * half_width, half_width, 1)
    flat_routes = routes.reshape(-1)
    onehot = (flat_routes[:, None] == jnp.arange(EXPERTS, dtype=jnp.int32)[None, :]).astype(
        jnp.int32
    )
    slots = jnp.sum((jnp.cumsum(onehot, axis=0) - 1) * onehot, axis=1)
    targets = (flat_routes * CAP + slots).reshape(tok_rows, TOP)
    slot_columns = jnp.arange(EXPERTS * CAP, dtype=jnp.int32)
    chosen = (targets[:, :, None] == slot_columns[None, None, :]).astype(jnp.float32)
    picker = jnp.sum(chosen, axis=1).astype(jnp.bfloat16)
    combine_weights = jnp.sum(chosen * route_weights[:, :, None], axis=1)
    contract_rows = (((0,), (0,)), ((), ()))
    own_half = lax.dynamic_slice_in_dim(moe_in, head_pos * half_width, half_width, 1)
    packed = lax.dot_general(
        picker, own_half, contract_rows, preferred_element_type=jnp.float32
    ).astype(jnp.bfloat16)
    chips = slices // head_count
    copies = jnp.broadcast_to(
        packed.reshape(EXPERTS, 1, CAP, half_width), (EXPERTS, chips, CAP, half_width)
    ).reshape(EXPERTS * chips, CAP, half_width)
    rows_in = dispatch(copies).reshape(-1, D)
    gate = jnp.dot(rows_in, w_gate, preferred_element_type=jnp.float32)
    upward = jnp.dot(rows_in, w_up, preferred_element_type=jnp.float32)
    inner = (jax.nn.silu(gate) * upward).astype(jnp.bfloat16)
    inner = lax.optimization_barrier(inner)
    part = jnp.dot(inner, w_down, preferred_element_type=jnp.float32).astype(jnp.bfloat16)
    back = combine(part.reshape(seq_count, CAP, D)).reshape(EXPERTS, chips, CAP, half_width)
    high = combine_weights.astype(jnp.bfloat16)
    low = (combine_weights - high.astype(jnp.float32)).astype(jnp.bfloat16)
    moe_out = jnp.zeros((tok_rows, half_width), jnp.float32)
    for chip in range(chips):
        piece = back[:, chip].reshape(EXPERTS * CAP, half_width)
        moe_out = moe_out + jnp.dot(high, piece, preferred_element_type=jnp.float32)
        moe_out = moe_out + jnp.dot(low, piece, preferred_element_type=jnp.float32)
    return (own_rows + moe_out).astype(jnp.bfloat16)


def solution(mesh):
    return jax.shard_map(
        per_device,
        mesh=mesh,
        in_specs=(
            P(("grp", "seq"), "head"),
            P(("grp", "seq"), "head"),
            P(("grp", "seq"), "head"),
            P(("grp", "seq"), "head"),
            P("head"),
            P("head", "seq"),
            P(),
            P(("grp", "seq"), None),
            P(("grp", "seq"), None),
            P(None, ("seq", "head")),
            P(None, ("seq", "head")),
            P(("seq", "head"), None),
        ),
        out_specs=P(("grp", "seq"), "head"),
        check_vma=False,
    )
```
